32 devices in a mesh: layer: 4 (over y, core), shard: 8 (over z, x).
Axes of the slice: x: 2, y: 2, z: 4, core: 2. Of those that a mesh axis runs over, the one named last changes fastest.
Arguments:
- input_acts: bfloat16 [8, 4096, 5120], P('layer', 'shard'), may hold values from -6 to 6
- output_grads: bfloat16 [8, 4096, 1024], P('layer', 'shard'), may hold values from -6 to 6
- input_inverse: bfloat16 [8, 5120, 5120], P('layer', 'shard'), may hold values from -1 to 2, as said below
- output_inverse: bfloat16 [8, 1024, 1024], P('layer', 'shard'), may hold values from -1 to 2, as said below
- query_input: bfloat16 [8, 5120, 512], P(None, 'shard'), may hold values from -0.0048828125 to 0.0048828125
- query_output: bfloat16 [8, 1024, 512], P(None, 'shard'), may hold values from -0.1875 to 0.1875
- layer_order: int32 [8], replicated, may hold values from 0 to 7, each once
Outputs:
- scores: float32 [4096, 16], P('shard', 'layer')
The draws below stay inside these ranges and needn't reach their ends.
Inputs may be any that keep to these rules, and one draw needn't show every extreme that they name: `input_inverse`: symmetric in its last two dimensions, with a unit-sized diagonal. `output_inverse`: symmetric in its last two dimensions, with a unit-sized diagonal.
All inputs are finite; a program needn't handle non-finite values.
Results may differ from the reference program's by a relative error of at most 0.0045.
Values may be sent and summed in bfloat16 or wider, within the bound.
No kernel may reach another device: no remote copies, remote signals or barrier semaphores. Data moves between devices by JAX's collectives and lax.ppermute only.
A program may use at most 128 MiB of HBM per device.

```python
import jax
import jax.numpy as jnp
from jax import lax

DIN = 5120
DOUT = 1024
QUERIES = 16
RANK = 32
LAYERS = 8
TOKENS = 4096


def symmetric_draw(key, width):
    raw = jax.random.truncated_normal(key, -4.0, 4.0, (LAYERS, width, width), jnp.float32)
    paired = (raw + jnp.swapaxes(raw, 1, 2)) * 0.7071
    result = jnp.eye(width, dtype=jnp.float32)[None] + 0.4 / jnp.sqrt(jnp.float32(width)) * paired
    return result.astype(jnp.bfloat16)


def draw_input_inverse(key, part):
    return symmetric_draw(jax.random.fold_in(key, 11), DIN)


def draw_output_inverse(key, part):
    return symmetric_draw(jax.random.fold_in(key, 13), DOUT)


def block_levels(stream_key, shape, cuts, least, top_value):
    gain = 1.0
    for dim, blocks in cuts:
        heights = jax.random.uniform(jax.random.fold_in(jax.random.fold_in(stream_key, 6), dim), (blocks,), jnp.float32, least / len(cuts), top_value / len(cuts))
        gain = gain * jnp.repeat(jnp.exp(heights), shape[dim] // blocks).reshape((-1,) + (1,) * (len(shape) - 1 - dim))
    return gain


def gaussian(own_key, dims, deviation, reach, split=(), kind=jnp.bfloat16):
    gain = block_levels(own_key, dims, split, -0.22, 0.18) if split else 1.0
    values = jax.random.normal(own_key, dims, jnp.float32) * deviation * gain
    return jnp.minimum(jnp.maximum(values, -reach), reach).astype(kind)


def setup_inputs(seed: int = 0) -> dict:
    key_of = jax.random.split(jax.random.key(seed), 8)
    return {
        "input_acts": gaussian(key_of[0], (LAYERS, TOKENS, DIN), 1.0, 6.0, ((0, 4), (1, 8))),
        "output_grads": gaussian(key_of[1], (LAYERS, TOKENS, DOUT), 1.0, 6.0, ((0, 4), (1, 8))),
        "input_inverse": draw_input_inverse(jax.random.fold_in(key_of[7], 71), 0),
        "output_inverse": draw_output_inverse(jax.random.fold_in(key_of[7], 71), 0),
        "query_input": gaussian(key_of[4], (LAYERS, DIN, QUERIES * RANK), (DIN * RANK * LAYERS) ** -0.5, 0.0048828125, ((1, 8),)),
        "query_output": gaussian(key_of[5], (LAYERS, DOUT, QUERIES * RANK), DOUT ** -0.5, 0.1875, ((1, 8),)),
        "layer_order": jax.random.permutation(key_of[6], LAYERS).astype(jnp.int32),
    }


def reference(input_acts, output_grads, input_inverse, output_inverse, query_input, query_output, layer_order):
    highest = lax.Precision.HIGHEST
    scores = jnp.zeros((TOKENS, QUERIES), jnp.float32)
    for position in range(LAYERS):
        model_layer = layer_order[position].astype(jnp.int32)
        vectors_in = lax.dynamic_index_in_dim(query_input, model_layer, 0, keepdims=False).astype(jnp.float32)
        vectors_out = lax.dynamic_index_in_dim(query_output, model_layer, 0, keepdims=False).astype(jnp.float32)
        folded_in = jnp.dot(input_inverse[position].astype(jnp.float32), vectors_in, precision=highest).astype(jnp.bfloat16)
        folded_out = jnp.dot(output_inverse[position].astype(jnp.float32), vectors_out, precision=highest).astype(jnp.bfloat16)
        left = jnp.dot(input_acts[position].astype(jnp.float32), folded_in.astype(jnp.float32), precision=highest)
        right = jnp.dot(output_grads[position].astype(jnp.float32), folded_out.astype(jnp.float32), precision=highest)
        scores = scores + (left * right).reshape(TOKENS, QUERIES, RANK).sum(axis=2)
    return scores
```

```python
import functools

import jax
import jax.numpy as jnp
from jax import lax
from jax.experimental import pallas as pl
from jax.experimental.pallas import tpu as pltpu
from jax.sharding import PartitionSpec as P

QUERIES = 16


def general(
    input_acts, output_grads, input_inverse, output_inverse, query_input, query_output, layer_order
):
    depth = input_acts.shape[0]
    tokens = input_acts.shape[1]
    first = lax.axis_index("layer") * depth
    chosen_in = []
    chosen_out = []
    for position in range(depth):
        model_layer = layer_order[first + position]
        chosen_in.append(lax.dynamic_index_in_dim(query_input, model_layer, 0, keepdims=False))
        chosen_out.append(lax.dynamic_index_in_dim(query_output, model_layer, 0, keepdims=False))
    vectors_in = jnp.stack(chosen_in, axis=1)
    vectors_out = jnp.stack(chosen_out, axis=1)
    width = vectors_in.shape[2]

    def side(rows, inverse, vectors):
        whole = lax.all_gather(vectors, "shard", axis=0, tiled=True)
        folded = jnp.einsum(
            "jsk,kjn->sjn", inverse, whole, preferred_element_type=jnp.float32
        ).astype(jnp.bfloat16)
        whole = lax.all_gather(folded, "shard", axis=0, tiled=True)
        return jnp.einsum("jti,ijn->jtn", rows, whole, preferred_element_type=jnp.float32)

    left = side(input_acts, input_inverse, vectors_in)
    right = side(output_grads, output_inverse, vectors_out)
    product = (left * right).reshape(depth, tokens, QUERIES, width // QUERIES).sum(axis=(0, 3))
    return lax.psum_scatter(product, "layer", scatter_dimension=1, tiled=True)


def pick_kernel(order, vectors_in, vectors_out, out):
    del order
    split = vectors_in.shape[1]
    out[0, :split] = vectors_in[0]
    out[0, split:] = vectors_out[0]


def pick(order, query_input, query_output):
    depth = order.shape[0]
    rows_in, width = query_input.shape[1:]
    rows_out = query_output.shape[1]
    return pl.pallas_call(
        pick_kernel,
        grid_spec=pltpu.PrefetchScalarGridSpec(
            num_scalar_prefetch=1,
            grid=(depth,),
            in_specs=[
                pl.BlockSpec((1, rows_in, width), lambda j, order: (order[j], 0, 0)),
                pl.BlockSpec((1, rows_out, width), lambda j, order: (order[j], 0, 0)),
            ],
            out_specs=pl.BlockSpec((1, rows_in + rows_out, width), lambda j, order: (j, 0, 0)),
        ),
        out_shape=jax.ShapeDtypeStruct((depth, rows_in + rows_out, width), query_input.dtype),
        name="pick",
    )(order, query_input, query_output)


def fold_kernel(count, guarded, resumed, last, control, *refs):
    wide = refs[:count]
    narrow = refs[count : 2 * count]
    blocks = refs[2 * count : 3 * count]
    refs = refs[3 * count :]
    if resumed:
        before_wide, before_narrow = refs[:2]
        refs = refs[2:]
    if last is None:
        total_wide, total_narrow = refs
    else:
        out, total_wide, total_narrow = refs
    split = wide[0].shape[2]
    fresh = not resumed
    if resumed:
        total_wide[0] = before_wide[0]
        total_narrow[0] = before_narrow[0]
    for i in range(count):

        def add(i=i, fresh=fresh):
            one = jnp.dot(wide[i][0], blocks[i][0, :split], preferred_element_type=jnp.float32)
            two = jnp.dot(narrow[i][0], blocks[i][0, split:], preferred_element_type=jnp.float32)
            if fresh:
                total_wide[0] = one
                total_narrow[0] = two
            else:
                total_wide[0] += one
                total_narrow[0] += two

        if guarded[i]:
            pl.when(control[count + i] != 0)(add)
        else:
            add()
            fresh = False
    if last == "round":
        rows = total_wide.shape[1]
        out[0, :rows] = total_wide[0].astype(out.dtype)
        out[0, rows:] = total_narrow[0].astype(out.dtype)
    elif last == "score":
        product = total_wide[0] * total_narrow[0]
        queries, width = out.shape[0], product.shape[1]
        owner = lax.broadcasted_iota(jnp.int32, (queries, width), 1) // (width // queries)
        row = lax.broadcasted_iota(jnp.int32, (queries, width), 0)
        sums = lax.dot_general(
            (owner == row).astype(jnp.float32),
            product,
            (((1,), (1,)), ((), ())),
            precision=lax.Precision.HIGHEST,
            preferred_element_type=jnp.float32,
        )

        @pl.when(pl.program_id(0) == 0)
        def _():
            out[...] = sums

        @pl.when(pl.program_id(0) != 0)
        def _():
            out[...] += sums


def fold(wide, narrow, pieces, before=None, last=None):
    count = len(pieces)
    depth, high, across = wide.shape
    low = narrow.shape[1]
    tall, width = pieces[0][0].shape[1:]
    share = across * tall // (across + narrow.shape[2])
    control = [owner for _, owner, _ in pieces]
    control += [True if valid is None else valid for _, _, valid in pieces]
    control = jnp.stack([jnp.asarray(c).astype(jnp.int32) for c in control])
    guarded = tuple(valid is not None for _, _, valid in pieces)
    assert before is not None or not guarded[0]

    def column(i):
        return lambda j, control: (j, 0, control[i])

    def layer(j, control):
        return (j, 0, 0)

    in_specs = [pl.BlockSpec((1, high, share), column(i)) for i in range(count)]
    in_specs += [pl.BlockSpec((1, low, tall - share), column(i)) for i in range(count)]
    in_specs += [pl.BlockSpec((1, tall, width), layer) for _ in range(count)]
    operands = [wide] * count + [narrow] * count + [shard for shard, _, _ in pieces]
    totals = [(1, high, width), (1, low, width)]
    if before is not None:
        in_specs += [pl.BlockSpec(shape, layer) for shape in totals]
        operands += list(before)
    scratch = []
    if last is None:
        out_specs = tuple(pl.BlockSpec(shape, layer) for shape in totals)
        out_shape = tuple(
            jax.ShapeDtypeStruct((depth,) + shape[1:], jnp.float32) for shape in totals
        )
    else:
        scratch = [pltpu.VMEM(shape, jnp.float32) for shape in totals]
        if last == "round":
            out_specs = pl.BlockSpec((1, high + low, width), layer)
            out_shape = jax.ShapeDtypeStruct((depth, high + low, width), jnp.bfloat16)
        else:
            out_specs = pl.BlockSpec((QUERIES, high), lambda j, control: (0, 0))
            out_shape = jax.ShapeDtypeStruct((QUERIES, high), jnp.float32)
    flops = 2 * depth * count * width * (high * share + low * (tall - share))
    moved = 2 * depth * count * (high * share + low * (tall - share) + tall * width)
    return pl.pallas_call(
        functools.partial(fold_kernel, count, guarded, before is not None, last),
        grid_spec=pltpu.PrefetchScalarGridSpec(
            num_scalar_prefetch=1,
            grid=(depth,),
            in_specs=in_specs,
            out_specs=out_specs,
            scratch_shapes=scratch,
        ),
        out_shape=out_shape,
        cost_estimate=pl.CostEstimate(
            flops=flops, bytes_accessed=moved + 8 * depth * (high + low) * width, transcendentals=0
        ),
        name="fold",
    )(control, *operands)


def swap(value, mask, among=None, axis="shard"):
    size = lax.axis_size(axis)
    pairs = [(s, s ^ mask) for s in range(size) if among is None or among(s)]
    return lax.ppermute(value, axis, pairs)


def is_end(s):
    return s >> 1 in (0, 3)


def is_middle(s):
    return not is_end(s)


def spread(own, wide, narrow, last):
    s = lax.axis_index("shard")
    end = (s >> 1 == 0) | (s >> 1 == 3)
    middle = ~end

    outer = swap(own, 2)
    inner = swap(own, 6, is_middle)
    pair = swap(own, 1)
    total = fold(wide, narrow, [(own, s, None)])

    carried = jnp.where(end, pair, inner)
    outer2 = swap(carried, 2)
    turn = lax.ppermute(
        outer,
        "shard",
        [(d, d ^ 1) if is_end(d) else (d, d ^ 6) for d in range(lax.axis_size("shard"))],
    )
    pair2 = swap(inner, 1, is_middle)
    total = fold(
        wide, narrow, [(outer, s ^ 2, None), (pair, s ^ 1, None), (inner, s ^ 6, middle)], total
    )

    outer3 = lax.ppermute(
        turn, "shard", [(d, d ^ 2) for d in range(lax.axis_size("shard")) if is_middle(d)]
    )
    turn2 = lax.ppermute(
        outer2,
        "shard",
        [(d, d ^ 1) if is_end(d) else (d, d ^ 6) for d in range(lax.axis_size("shard"))],
    )
    total = fold(
        wide,
        narrow,
        [
            (outer2, jnp.where(end, s ^ 4, s ^ 3), None),
            (turn, jnp.where(end, s ^ 3, s ^ 4), None),
            (pair2, s ^ 7, middle),
        ],
        total,
    )
    pair3 = swap(outer3, 1, is_end)
    total = fold(wide, narrow, [(turn2, s ^ 5, None), (outer3, s ^ 6, end)], total)
    return fold(wide, narrow, [(pair3, s ^ 7, end)], total, last)


def gridded(
    input_acts, output_grads, input_inverse, output_inverse, query_input, query_output, layer_order
):
    depth = input_acts.shape[0]
    layer = lax.axis_index("layer")
    order = lax.dynamic_slice_in_dim(layer_order, layer * depth, depth)
    own = pick(order, query_input, query_output)
    folded = spread(own, input_inverse, output_inverse, "round")
    scores = spread(folded, input_acts, output_grads, "score")
    mask = lax.axis_size("layer")
    while mask > 1:
        mask //= 2
        half = scores.shape[0] // 2
        upper = (layer & mask) != 0
        low, high = scores[:half], scores[half:]
        scores = jnp.where(upper, high, low) + swap(
            jnp.where(upper, low, high), mask, axis="layer"
        )
    return scores.T


def solution(mesh):
    in_specs = (
        P("layer", "shard", None),
        P("layer", "shard", None),
        P("layer", "shard", None),
        P("layer", "shard", None),
        P(None, "shard", None),
        P(None, "shard", None),
        P(),
    )
    out_specs = P("shard", "layer")
    layers = mesh.shape["layer"]
    fits = mesh.shape["shard"] == 8 and layers & (layers - 1) == 0 and QUERIES % layers == 0
    return jax.shard_map(
        gridded if fits else general,
        mesh=mesh,
        in_specs=in_specs,
        out_specs=out_specs,
        check_vma=False,
    )
```
